256 devices in a mesh: dp: 32 (over z, y), seq: 8 (over x, core).
Axes of the slice: x: 4, y: 4, z: 8, core: 2. Of those that a mesh axis runs over, the one named last changes fastest.
Arguments:
- prefill_queries: bfloat16 [32768, 4096], P(('dp', 'seq')), may hold values from -8 to 8
- prefill_key_values: bfloat16 [32768, 2048], P(('dp', 'seq')), may hold values from -8 to 8
- decode_queries: bfloat16 [32, 4096], P('dp', 'seq'), may hold values from -8 to 8
- decode_key_values: bfloat16 [32, 2048], P('dp', 'seq'), may hold values from -8 to 8
- arrival: int32 [32], replicated, may hold values from 0 to 31, as said below
- pooled_key_values: bfloat16 [1024, 128, 2048], P('dp', None, 'seq'), may hold values from -8 to 8
- page_table: int32 [32, 32], P('dp'), may hold values from 0 to 31, as said below
- cache_len: int32 [32], P('dp'), may hold values from 1 to 4096, as said below
- mover: int32 [32], P('dp'), may hold values from 0 to 0, as said below
Outputs:
- prefill_out: bfloat16 [32768, 4096], P(('dp', 'seq'))
- decode_out: bfloat16 [32, 4096], P('dp', 'seq')
- received_pages: bfloat16 [1024, 128, 2048], P('dp', None, 'seq')
The draws below stay inside these ranges and needn't reach their ends.
Inputs may be any that keep to these rules, and one draw needn't show every extreme that they name: `arrival`: every decode request appears exactly once. `page_table`: the 1 request of one group together name each of that group's 32 pages exactly once. `cache_len`: some request has exactly 4096 cached tokens in every draw. `mover`: the request with the most cached tokens always moves.
All inputs are finite; a program needn't handle non-finite values.
Results may differ from the reference program's by a relative error of at most 0.006.
Values may be sent and summed in bfloat16 or wider, within the bound.
A program may use at most 64 MiB of HBM per device.

```python
import math
import jax
import jax.numpy as jnp
from jax import lax

QUERY_HEADS = 32
KV_HEAD_COUNT = 8
HEAD_SIZE = 128
PREFILL_LENGTH = 1024
REQ_GRP = 1
MOST_CACHED = 4096
PAGE_TOKENS = 128
PAGES_REQ = 32
GROUP_PAGES = 32
REQUEST_GROUPS = 32
DECODE_REQUESTS = 32
PREFILL_TOTAL = 32768
MOVED_ROWS_TOTAL = 1024


def starting_values(key, shape):
    return jnp.clip(jax.random.normal(key, shape, jnp.float32), -6.0, 6.0)


def top_request(key):
    return jax.random.randint(jax.random.fold_in(key, 31), (), 0, DECODE_REQUESTS)


def lengths_of(key):
    base_key = jax.random.fold_in(key, 32)
    first_key, second_key, third_key, fourth_key = jax.random.split(base_key, 4)
    raw_lengths = jax.random.randint(first_key, (DECODE_REQUESTS,), MOST_CACHED // 8, MOST_CACHED + 1)
    shifts = jax.random.randint(second_key, (DECODE_REQUESTS,), 0, 2)
    lengths_all = jnp.maximum(jnp.right_shift(raw_lengths, shifts), 1)
    longest = top_request(key)
    shortest = (longest + 1 + jax.random.randint(third_key, (), 0, max(DECODE_REQUESTS - 1, 1))) % DECODE_REQUESTS
    lengths_all = lengths_all.at[shortest].set(jax.random.randint(fourth_key, (), 1, 5))
    lengths_all = lengths_all.at[longest].set(MOST_CACHED)
    return lengths_all.astype(jnp.int32)


def permute_pool(pool_key):
    return jax.random.permutation(pool_key, GROUP_PAGES)


def table_of(key):
    group_number = DECODE_REQUESTS // REQ_GRP
    group_keys = jax.random.split(jax.random.fold_in(key, 34), group_number)
    orders = jax.vmap(permute_pool)(group_keys)
    return orders.reshape(DECODE_REQUESTS, PAGES_REQ).astype(jnp.int32)


def arrival_of(key):
    return jax.random.permutation(jax.random.fold_in(key, 35), DECODE_REQUESTS).astype(jnp.int32)


def draw_arrival(key, part):
    return arrival_of(key)


def draw_cache_len(key, part):
    return lengths_of(key)


def draw_page_table(key, part):
    return table_of(key)


def draw_mover(key, part):
    group_number = DECODE_REQUESTS // REQ_GRP
    slots = jax.random.randint(jax.random.fold_in(key, 33), (group_number,), 0, REQ_GRP)
    longest = top_request(key)
    slots = slots.at[longest // REQ_GRP].set(longest % REQ_GRP)
    return slots.astype(jnp.int32)


def prefill_pair(key):
    group_extent = QUERY_HEADS // KV_HEAD_COUNT
    query_entries = starting_values(jax.random.fold_in(key, 41), (PREFILL_TOTAL, KV_HEAD_COUNT, group_extent, HEAD_SIZE))
    key_value_entries = starting_values(jax.random.fold_in(key, 42), (PREFILL_TOTAL, KV_HEAD_COUNT, 2, HEAD_SIZE))
    return (query_entries.reshape(PREFILL_TOTAL, QUERY_HEADS * HEAD_SIZE), key_value_entries.reshape(PREFILL_TOTAL, KV_HEAD_COUNT * 2 * HEAD_SIZE))


def draw_prefill_queries(key, part):
    return prefill_pair(key)[0].astype(jnp.bfloat16)


def draw_prefill_key_values(key, part):
    return prefill_pair(key)[1].astype(jnp.bfloat16)


def decode_set(key):
    group_number = DECODE_REQUESTS // REQ_GRP
    group_extent = QUERY_HEADS // KV_HEAD_COUNT
    query_entries = starting_values(jax.random.fold_in(key, 51), (DECODE_REQUESTS, KV_HEAD_COUNT, group_extent, HEAD_SIZE))
    key_value_entries = starting_values(jax.random.fold_in(key, 52), (DECODE_REQUESTS, KV_HEAD_COUNT, 2, HEAD_SIZE))
    pooled_entries = starting_values(jax.random.fold_in(key, 53), (group_number * GROUP_PAGES, PAGE_TOKENS, KV_HEAD_COUNT, 2, HEAD_SIZE))
    return (query_entries.reshape(DECODE_REQUESTS, QUERY_HEADS * HEAD_SIZE), key_value_entries.reshape(DECODE_REQUESTS, KV_HEAD_COUNT * 2 * HEAD_SIZE), pooled_entries.reshape(group_number * GROUP_PAGES, PAGE_TOKENS, KV_HEAD_COUNT * 2 * HEAD_SIZE))


def draw_decode_queries(key, part):
    return decode_set(key)[0].astype(jnp.bfloat16)


def draw_decode_key_values(key, part):
    return decode_set(key)[1].astype(jnp.bfloat16)


def draw_pooled_key_values(key, part):
    return decode_set(key)[2].astype(jnp.bfloat16)


def setup_inputs(seed: int = 0) -> dict:
    seeds = jax.random.split(jax.random.key(seed), 10)
    return {
        "prefill_queries": draw_prefill_queries(jax.random.fold_in(seeds[9], 71), 0),
        "prefill_key_values": draw_prefill_key_values(jax.random.fold_in(seeds[9], 71), 0),
        "decode_queries": draw_decode_queries(jax.random.fold_in(seeds[9], 71), 0),
        "decode_key_values": draw_decode_key_values(jax.random.fold_in(seeds[9], 71), 0),
        "arrival": draw_arrival(jax.random.fold_in(seeds[9], 71), 0),
        "pooled_key_values": draw_pooled_key_values(jax.random.fold_in(seeds[9], 71), 0),
        "page_table": draw_page_table(jax.random.fold_in(seeds[9], 71), 0),
        "cache_len": draw_cache_len(jax.random.fold_in(seeds[9], 71), 0),
        "mover": draw_mover(jax.random.fold_in(seeds[9], 71), 0),
    }


NEG_FILL = -1e+30

def prefill_sequence(query_sequence, key_value_sequence):
    group_extent = QUERY_HEADS // KV_HEAD_COUNT
    query_rows = query_sequence.astype(jnp.float32).reshape(PREFILL_LENGTH, KV_HEAD_COUNT, group_extent, HEAD_SIZE)
    key_value_rows = key_value_sequence.astype(jnp.float32).reshape(PREFILL_LENGTH, KV_HEAD_COUNT, 2 * HEAD_SIZE)
    key_part = key_value_rows[:, :, :HEAD_SIZE]
    value_part = key_value_rows[:, :, HEAD_SIZE:]
    scale_factor = 1.0 / math.sqrt(HEAD_SIZE)
    block_rows = min(512, PREFILL_LENGTH)
    results = []
    for block_index in range(PREFILL_LENGTH // block_rows):
        first_row = block_index * block_rows
        last_key = first_row + block_rows
        scores = jnp.einsum('qngd,knd->ngqk', query_rows[first_row:last_key], key_part[:last_key]) * scale_factor
        row_pos = first_row + lax.broadcasted_iota(jnp.int32, (block_rows, last_key), 0)
        key_pos = lax.broadcasted_iota(jnp.int32, (block_rows, last_key), 1)
        allowed = key_pos <= row_pos
        masked = jnp.where(allowed, scores, NEG_FILL)
        row_max = lax.optimization_barrier(jnp.max(masked, axis=-1, keepdims=True))
        weights = jnp.where(allowed, jnp.exp(masked - row_max), 0.0).astype(jnp.bfloat16)
        wide_weights = weights.astype(jnp.float32)
        totals = lax.optimization_barrier(jnp.sum(wide_weights, axis=-1))
        summed = jnp.einsum('ngqk,knd->qngd', wide_weights, value_part[:last_key])
        normed = summed / jnp.transpose(totals, (2, 0, 1))[..., None]
        results.append(normed.astype(jnp.bfloat16).reshape(block_rows, QUERY_HEADS * HEAD_SIZE))
    return jnp.concatenate(results, axis=0)

def sequence_pair(pair_args):
    return prefill_sequence(pair_args[0], pair_args[1])

def reference(prefill_queries, prefill_key_values, decode_queries, decode_key_values, arrival, pooled_key_values, page_table, cache_len, mover):
    query_groups = prefill_queries.reshape(REQUEST_GROUPS, PREFILL_LENGTH, QUERY_HEADS * HEAD_SIZE)
    key_value_groups = prefill_key_values.reshape(REQUEST_GROUPS, PREFILL_LENGTH, KV_HEAD_COUNT * 2 * HEAD_SIZE)
    prefill_out = lax.map(sequence_pair, (query_groups, key_value_groups)).reshape(PREFILL_TOTAL, QUERY_HEADS * HEAD_SIZE)
    group_extent = QUERY_HEADS // KV_HEAD_COUNT
    scale_factor = 1.0 / math.sqrt(HEAD_SIZE)
    decode_row = jnp.zeros((DECODE_REQUESTS,), jnp.int32).at[arrival].set(jnp.arange(DECODE_REQUESTS, dtype=jnp.int32))

    def one_request(request):
        group_id = request // REQ_GRP
        index_of_row = decode_row[request]
        single_query = decode_queries[index_of_row].astype(jnp.float32).reshape(KV_HEAD_COUNT, group_extent, HEAD_SIZE)
        single_key_value = decode_key_values[index_of_row].astype(jnp.float32).reshape(KV_HEAD_COUNT, 2 * HEAD_SIZE)
        page_numbers = group_id * GROUP_PAGES + page_table[request]
        cache_row_list = pooled_key_values[page_numbers].astype(jnp.float32).reshape(MOST_CACHED, KV_HEAD_COUNT, 2 * HEAD_SIZE)
        cached_scores = jnp.einsum('ngd,tnd->ngt', single_query, cache_row_list[:, :, :HEAD_SIZE]) * scale_factor
        new_scores = jnp.einsum('ngd,nd->ng', single_query, single_key_value[:, :HEAD_SIZE]) * scale_factor
        valid_rows = jnp.arange(MOST_CACHED) < cache_len[request]
        masked = jnp.where(valid_rows, cached_scores, NEG_FILL)
        row_max = jnp.maximum(lax.optimization_barrier(jnp.max(masked, axis=-1)), new_scores)
        cached_weights = jnp.where(valid_rows, jnp.exp(masked - row_max[..., None]), 0.0).astype(jnp.bfloat16)
        new_weights = jnp.exp(new_scores - row_max).astype(jnp.bfloat16)
        wide_cached = cached_weights.astype(jnp.float32)
        wide_new = new_weights.astype(jnp.float32)
        totals = lax.optimization_barrier(jnp.sum(wide_cached, axis=-1)) + wide_new
        summed = jnp.einsum('ngt,tnd->ngd', wide_cached, cache_row_list[:, :, HEAD_SIZE:])
        summed = summed + wide_new[..., None] * single_key_value[:, None, HEAD_SIZE:]
        return (summed / totals[..., None]).astype(jnp.bfloat16).reshape(QUERY_HEADS * HEAD_SIZE)
    decode_out = lax.map(one_request, jnp.arange(DECODE_REQUESTS, dtype=jnp.int32))

    def receiving_group(target):
        source = (target + REQUEST_GROUPS - 1) % REQUEST_GROUPS
        request = source * REQ_GRP + mover[source]
        page_rows = pooled_key_values[source * GROUP_PAGES + page_table[request]]
        live_pages = jnp.arange(PAGES_REQ) * PAGE_TOKENS < cache_len[request]
        return jnp.where(live_pages[:, None, None], page_rows, jnp.zeros_like(page_rows))
    received_pages = lax.map(receiving_group, jnp.arange(REQUEST_GROUPS, dtype=jnp.int32)).reshape(MOVED_ROWS_TOTAL, PAGE_TOKENS, KV_HEAD_COUNT * 2 * HEAD_SIZE)
    return (prefill_out, decode_out, received_pages)
```

```python
import functools
import math

import jax
import jax.numpy as jnp
from jax import lax
from jax.experimental import pallas as pl
from jax.experimental.pallas import tpu as pltpu
from jax.sharding import PartitionSpec as P

QUERY_HEADS = 32
KV_HEAD_COUNT = 8
HEAD_SIZE = 128
GROUP_EXTENT = QUERY_HEADS // KV_HEAD_COUNT
NEG_FILL = -1e30
SCALE = 1.0 / math.sqrt(HEAD_SIZE)
MESH = pl.DeviceIdType.MESH
Y_CHIPS = 4
Z_CHIPS = 8
HALF = 64


def exchange_kernel(
    kv_ref,
    query_ref,
    pair_ref,
    table_ref,
    len_ref,
    all_kv_ref,
    all_query_ref,
    all_pair_ref,
    near_table_ref,
    near_len_ref,
    kv_recv,
    kv_send,
    part_recv,
    part_send,
    own_sem,
    row_recv,
    row_send,
    block_recv,
    block_send,
    meta_recv,
    meta_send,
):
    group = lax.axis_index("dp")
    member = lax.axis_index("seq")
    z, y = group // Y_CHIPS, group % Y_CHIPS
    x, core = member // 2, member % 2
    next_group = (group + 1) % (Y_CHIPS * Z_CHIPS)

    def at(g, m):
        return (g, m)

    peers = [at(group, 2 * x + 1 - core)]
    for hop in (1, 3):
        peers.append(at(group, 2 * ((x + hop) % 4) + core))
    for hop in range(1, Y_CHIPS):
        peers.append(at(z * Y_CHIPS + (y + hop) % Y_CHIPS, member))
    for hop in range(1, Z_CHIPS):
        peers.append(at(((z + hop) % Z_CHIPS) * Y_CHIPS + y, member))
    previous_group = (group + Y_CHIPS * Z_CHIPS - 1) % (Y_CHIPS * Z_CHIPS)
    peers.append(at(next_group, member))
    peers.append(at(previous_group, member))
    barrier = pltpu.get_barrier_semaphore()
    for peer in peers:
        pl.semaphore_signal(barrier, inc=1, device_id=peer, device_id_type=MESH)
    pl.semaphore_wait(barrier, len(peers))

    def kv_copy(source, chip, half, target, lane):
        rows = pl.ds(half * HALF, HALF)
        return pltpu.make_async_remote_copy(
            src_ref=source.at[rows],
            dst_ref=all_kv_ref.at[2 * chip + core, rows],
            send_sem=kv_send.at[lane],
            recv_sem=kv_recv.at[chip, half],
            device_id=target,
            device_id_type=MESH,
        )

    def part_copy(source, chip, half):
        rows = pl.ds(half * HALF, HALF)
        return pltpu.make_async_remote_copy(
            src_ref=source.at[rows],
            dst_ref=all_kv_ref.at[2 * chip + core, rows],
            send_sem=part_send.at[chip, half],
            recv_sem=part_recv.at[chip, half],
            device_id=at(group, 2 * x + 1 - core),
            device_id_type=MESH,
        )

    def chip_at(c):
        return at(group, 2 * c + core)

    def held(chip):
        return all_kv_ref.at[2 * chip + core]

    @pl.when(x < 3)
    def _():
        for half in range(2):
            kv_copy(kv_ref, x, half, chip_at(x + 1), half).start()

    @pl.when(x == 0)
    def _():
        for half in range(2):
            kv_copy(kv_ref, x, half, chip_at(3), 2 + half).start()

    @pl.when(x == 1)
    def _():
        kv_copy(kv_ref, x, 1, chip_at(0), 2).start()

    for half in range(2):
        part_copy(kv_ref, x, half).start()
    own = pltpu.make_async_copy(kv_ref, all_kv_ref.at[member], own_sem)
    own.start()

    metas = []
    for index, (source, target) in enumerate(
        ((table_ref, near_table_ref), (len_ref, near_len_ref))
    ):
        metas.append(
            pltpu.make_async_remote_copy(
                src_ref=source,
                dst_ref=target,
                send_sem=meta_send.at[index],
                recv_sem=meta_recv.at[index],
                device_id=at(next_group, member),
                device_id_type=MESH,
            )
        )
        metas[-1].start()

    rows_out = []
    for index, (source, target) in enumerate(
        ((query_ref, all_query_ref), (pair_ref, all_pair_ref))
    ):
        mine = pltpu.make_async_copy(source, target.at[z, y], row_recv.at[index, 0])
        mine.start()
        rows_out.append(mine)
        for hop in range(1, Y_CHIPS):
            copy = pltpu.make_async_remote_copy(
                src_ref=source,
                dst_ref=target.at[z, y],
                send_sem=row_send.at[index, hop],
                recv_sem=row_recv.at[index, hop],
                device_id=at(z * Y_CHIPS + (y + hop) % Y_CHIPS, member),
                device_id_type=MESH,
            )
            copy.start()
            rows_out.append(copy)
    for copy in rows_out:
        copy.wait()
    blocks_out = []
    for index, target in enumerate((all_query_ref, all_pair_ref)):
        for hop in range(1, Z_CHIPS):
            copy = pltpu.make_async_remote_copy(
                src_ref=target.at[z],
                dst_ref=target.at[z],
                send_sem=block_send.at[index, hop],
                recv_sem=block_recv.at[index, hop],
                device_id=at(((z + hop) % Z_CHIPS) * Y_CHIPS + y, member),
                device_id_type=MESH,
            )
            copy.start()
            blocks_out.append(copy)

    def arrived(chip, half):
        kv_copy(kv_ref, chip, half, chip_at(0), 0).wait_recv()

    @pl.when(x == 0)
    def _():
        arrived(1, 1)
        kv_copy(held(1), 1, 1, chip_at(3), 4).start()
        for lane in range(5):
            kv_copy(kv_ref, x, 0, chip_at(1), lane).wait_send()

    @pl.when(x == 1)
    def _():
        for half in range(2):
            arrived(0, half)
            part_copy(held(0), 0, half).start()
        for lane in range(3):
            kv_copy(kv_ref, x, 0, chip_at(0), lane).wait_send()

    @pl.when(x == 2)
    def _():
        arrived(1, 0)
        kv_copy(held(1), 1, 0, chip_at(3), 2).start()
        part_copy(held(1), 1, 0).start()
        arrived(1, 1)
        part_copy(held(1), 1, 1).start()
        for half in range(2):
            arrived(0, half)
            part_copy(held(0), 0, half).start()
        for lane in range(3):
            kv_copy(kv_ref, x, 0, chip_at(3), lane).wait_send()

    @pl.when(x == 3)
    def _():
        for half in range(2):
            arrived(0, half)
            kv_copy(held(0), 0, half, chip_at(2), half).start()
            part_copy(held(0), 0, half).start()
            arrived(2, half)
            part_copy(held(2), 2, half).start()
        for half in range(2):
            arrived(1, half)
            part_copy(held(1), 1, half).start()
        for lane in range(2):
            kv_copy(kv_ref, x, 0, chip_at(2), lane).wait_send()

    for chip in range(4):

        @pl.when(chip <= x)
        def _():
            for half in range(2):
                part_copy(kv_ref, chip, half).wait()

    for copy in blocks_out + metas:
        copy.wait()
    own.wait()


def exchange(kv, query, pair, table, lens):
    any_space = pl.BlockSpec(memory_space=pl.ANY)
    dma = pltpu.SemaphoreType.DMA
    return pl.pallas_call(
        exchange_kernel,
        out_shape=(
            jax.ShapeDtypeStruct((8,) + kv.shape, kv.dtype),
            jax.ShapeDtypeStruct((Z_CHIPS, Y_CHIPS) + query.shape, query.dtype),
            jax.ShapeDtypeStruct((Z_CHIPS, Y_CHIPS) + pair.shape, pair.dtype),
            jax.ShapeDtypeStruct(table.shape, table.dtype),
            jax.ShapeDtypeStruct(lens.shape, lens.dtype),
        ),
        in_specs=[any_space] * 5,
        out_specs=(any_space,) * 5,
        scratch_shapes=[
            dma((4, 2)),
            dma((5,)),
            dma((4, 2)),
            dma((4, 2)),
            dma,
            dma((2, 4)),
            dma((2, 4)),
            dma((2, 8)),
            dma((2, 8)),
            dma((2,)),
            dma((2,)),
        ],
        compiler_params=pltpu.CompilerParams(collective_id=0, has_side_effects=True),
        name="exchange",
    )(kv, query, pair, table, lens)


def prefill_kernel(query_ref, kv_ref, out_ref):
    member = lax.axis_index("seq")
    x, core = member // 2, member % 2
    rows = query_ref.shape[0]

    def attend(chips):
        keys = 256 * chips
        key = kv_ref[:keys, :HEAD_SIZE]
        value = jnp.concatenate(
            [kv_ref[:keys, HEAD_SIZE:], jnp.ones((keys, HEAD_SIZE), jnp.bfloat16)], axis=1
        )
        allowed = lax.broadcasted_iota(jnp.int32, (rows, 256), 1) <= (
            core * 128 + lax.broadcasted_iota(jnp.int32, (rows, 256), 0)
        )
        for g in range(GROUP_EXTENT):
            columns = slice(g * HEAD_SIZE, (g + 1) * HEAD_SIZE)
            scores = lax.dot_general(
                query_ref[:, columns],
                key,
                (((1,), (1,)), ((), ())),
                preferred_element_type=jnp.float32,
            )
            last = jnp.where(allowed, scores[:, keys - 256 :], NEG_FILL)
            if chips > 1:
                scores = jnp.concatenate([scores[:, : keys - 256], last], axis=1)
            else:
                scores = last
            top = jnp.max(scores, axis=1, keepdims=True)
            weights = jnp.exp((scores - top) * SCALE).astype(jnp.bfloat16)
            summed = jnp.dot(weights, value, preferred_element_type=jnp.float32)
            out_ref[:, columns] = (summed[:, :HEAD_SIZE] / summed[:, HEAD_SIZE:]).astype(
                jnp.bfloat16
            )

    for chips in range(1, 5):
        pl.when(x == chips - 1)(functools.partial(attend, chips))


def prefill(query, all_kv):
    rows = query.shape[0]
    return pl.pallas_call(
        prefill_kernel,
        grid=(KV_HEAD_COUNT,),
        out_shape=jax.ShapeDtypeStruct(query.shape, query.dtype),
        in_specs=[
            pl.BlockSpec((rows, GROUP_EXTENT * HEAD_SIZE), lambda n: (0, n)),
            pl.BlockSpec((all_kv.shape[0], 2 * HEAD_SIZE), lambda n: (0, n)),
        ],
        out_specs=pl.BlockSpec((rows, GROUP_EXTENT * HEAD_SIZE), lambda n: (0, n)),
        cost_estimate=pl.CostEstimate(
            flops=4 * rows * 1024 * QUERY_HEADS * HEAD_SIZE,
            bytes_accessed=6 << 20,
            transcendentals=rows * 1024 * QUERY_HEADS,
        ),
        name="prefill",
    )(query, all_kv)


def decode_kernel(
    arrival_ref, table_ref, len_ref, query_ref, pair_ref, pool_ref, out_ref, cache_ref, sems
):
    pages, tokens = pool_ref.shape[0], pool_ref.shape[1]
    cached = pages * tokens
    copies = []
    for i in range(pages):
        copies.append(
            pltpu.make_async_copy(
                pool_ref.at[table_ref[0, i]],
                cache_ref.at[pl.ds(i * tokens, tokens)],
                sems.at[i],
            )
        )
        copies[-1].start()
    me = lax.axis_index("dp")
    row = jnp.int32(0)
    for i in range(arrival_ref.shape[0]):
        row = jnp.where(arrival_ref[i] == me, i, row)
    flat = query_ref[row].astype(jnp.float32)
    query = jnp.concatenate(
        [flat[:, g * HEAD_SIZE : (g + 1) * HEAD_SIZE] for g in range(GROUP_EXTENT)]
        + [jnp.zeros((8 - GROUP_EXTENT, HEAD_SIZE), jnp.float32)],
        axis=0,
    ).astype(jnp.bfloat16)
    pair = jnp.broadcast_to(pair_ref[row].astype(jnp.float32), (tokens, 2 * HEAD_SIZE))
    first = lax.broadcasted_iota(jnp.int32, pair.shape, 0) == 0
    cache_ref[cached:, :] = jnp.where(first, pair, 0.0).astype(jnp.bfloat16)
    for copy in copies:
        copy.wait()
    scores = lax.dot_general(
        query,
        cache_ref[:, :HEAD_SIZE],
        (((1,), (1,)), ((), ())),
        preferred_element_type=jnp.float32,
    )
    spot = lax.broadcasted_iota(jnp.int32, scores.shape, 1)
    scores = jnp.where((spot < len_ref[0]) | (spot == cached), scores, NEG_FILL)
    top = jnp.max(scores, axis=1, keepdims=True)
    weights = jnp.exp((scores - top) * SCALE).astype(jnp.bfloat16)
    value = jnp.concatenate(
        [cache_ref[:, HEAD_SIZE:], jnp.ones((cached + tokens, HEAD_SIZE), jnp.bfloat16)], axis=1
    )
    summed = jnp.dot(weights, value, preferred_element_type=jnp.float32)
    normed = summed[:, :HEAD_SIZE] / summed[:, HEAD_SIZE:]
    for g in range(GROUP_EXTENT):
        out_ref[:, g * HEAD_SIZE : (g + 1) * HEAD_SIZE] = normed[g : g + 1].astype(jnp.bfloat16)


def decode(arrival, table, lens, query, pair, pool):
    pages, tokens, width = pool.shape
    smem = pl.BlockSpec(memory_space=pltpu.SMEM)
    vmem = pl.BlockSpec(memory_space=pltpu.VMEM)
    return pl.pallas_call(
        decode_kernel,
        out_shape=jax.ShapeDtypeStruct((1, query.shape[-1]), jnp.bfloat16),
        in_specs=[smem, smem, smem, vmem, vmem, pl.BlockSpec(memory_space=pl.ANY)],
        out_specs=vmem,
        scratch_shapes=[
            pltpu.VMEM(((pages + 1) * tokens, width), jnp.bfloat16),
            pltpu.SemaphoreType.DMA((pages,)),
        ],
        cost_estimate=pl.CostEstimate(
            flops=1 << 27, bytes_accessed=2 << 20, transcendentals=1 << 15
        ),
        name="decode",
    )(arrival, table, lens, query, pair, pool)


def place_kernel(table_ref, len_ref, raw_ref, out_ref, held_ref, zero_ref, in_sems, out_sems):
    pages, tokens = raw_ref.shape[0], raw_ref.shape[1]
    for i in range(pages):
        pltpu.make_async_copy(
            raw_ref.at[table_ref[0, i]], held_ref.at[i], in_sems.at[i]
        ).start()
    zero_ref[...] = jnp.zeros_like(zero_ref)
    for i in range(pages):
        pltpu.make_async_copy(raw_ref.at[0], held_ref.at[i], in_sems.at[i]).wait()
        live = i * tokens < len_ref[0]

        @pl.when(live)
        def _():
            pltpu.make_async_copy(held_ref.at[i], out_ref.at[i], out_sems.at[i]).start()

        @pl.when(jnp.logical_not(live))
        def _():
            pltpu.make_async_copy(zero_ref, out_ref.at[i], out_sems.at[i]).start()

    for i in range(pages):
        pltpu.make_async_copy(zero_ref, out_ref.at[i], out_sems.at[i]).wait()


def place_pages(table, lens, raw):
    pages = raw.shape[0]
    smem = pl.BlockSpec(memory_space=pltpu.SMEM)
    any_space = pl.BlockSpec(memory_space=pl.ANY)
    return pl.pallas_call(
        place_kernel,
        out_shape=jax.ShapeDtypeStruct(raw.shape, raw.dtype),
        in_specs=[smem, smem, any_space],
        out_specs=any_space,
        scratch_shapes=[
            pltpu.VMEM(raw.shape, raw.dtype),
            pltpu.VMEM(raw.shape[1:], raw.dtype),
            pltpu.SemaphoreType.DMA((pages,)),
            pltpu.SemaphoreType.DMA((pages,)),
        ],
        cost_estimate=pl.CostEstimate(flops=0, bytes_accessed=4 << 20, transcendentals=0),
        name="place_pages",
    )(table, lens, raw)


def on_device(
    prefill_queries,
    prefill_key_values,
    decode_queries,
    decode_key_values,
    arrival,
    pooled_key_values,
    page_table,
    cache_len,
    mover,
):
    groups = lax.axis_size("dp")
    raw = lax.ppermute(
        pooled_key_values, "dp", [((i - 1) % groups, i) for i in range(groups)]
    )
    moving_table = lax.dynamic_slice_in_dim(page_table, mover[0], 1, 0)
    moving_len = lax.dynamic_slice_in_dim(cache_len, mover[0], 1, 0)
    all_kv, all_query, all_pair, near_table, near_len = exchange(
        prefill_key_values, decode_queries, decode_key_values, moving_table, moving_len
    )
    prefill_out = prefill(prefill_queries, all_kv.reshape(-1, all_kv.shape[-1]))
    decode_out = decode(
        arrival,
        page_table,
        cache_len,
        all_query.reshape((groups,) + decode_queries.shape),
        all_pair.reshape((groups,) + decode_key_values.shape),
        pooled_key_values,
    )
    received_pages = place_pages(near_table, near_len, raw)
    return (prefill_out, decode_out, received_pages)


def solution(mesh):
    placed = (
        P(("dp", "seq"), None),
        P(("dp", "seq"), None),
        P("dp", "seq"),
        P("dp", "seq"),
        P(),
        P("dp", None, "seq"),
        P("dp", None),
        P("dp"),
        P("dp"),
    )
    return jax.shard_map(
        on_device,
        mesh=mesh,
        in_specs=placed,
        out_specs=(P(("dp", "seq"), None), P("dp", "seq"), P("dp", None, "seq")),
        check_vma=False,
    )
```

```python
import functools
import math

import jax
import jax.numpy as jnp
from jax import lax
from jax.experimental import pallas as pl
from jax.experimental.pallas import tpu as pltpu
from jax.sharding import PartitionSpec as P

QUERY_HEADS = 32
KV_HEAD_COUNT = 8
HEAD_SIZE = 128
GROUP_EXTENT = QUERY_HEADS // KV_HEAD_COUNT
NEG_FILL = -1e30
SCALE = 1.0 / math.sqrt(HEAD_SIZE)
MESH = pl.DeviceIdType.MESH
Y_CHIPS = 4
Z_CHIPS = 8
HALF = 64
FORWARD_PAGES = 24
PIECES = 2


def exact_dot(left, right, dimensions):
    return lax.dot_general(
        left, right, (dimensions, ((), ())), preferred_element_type=jnp.float32
    )


def main_kernel(
    arrival_ref,
    table_ref,
    len_ref,
    query_ref,
    kv_ref,
    row_query_ref,
    row_pair_ref,
    pool_ref,
    move_table_ref,
    move_len_ref,
    prefill_ref,
    decode_ref,
    raw_ref,
    near_table_ref,
    near_len_ref,
    queries,
    kv_all,
    pool,
    outs,
    all_query,
    all_pair,
    decode_out,
    relays,
    load_sems,
    out_sems,
    kv_recv,
    kv_send,
    part_recv,
    part_send,
    row_recv,
    row_send,
    meta_recv,
    meta_send,
    page_recv,
    page_send,
    relay_recv,
    relay_send,
):
    group = lax.axis_index("dp")
    member = lax.axis_index("seq")
    z, y = group // Y_CHIPS, group % Y_CHIPS
    x, core = member // 2, member % 2
    groups = Y_CHIPS * Z_CHIPS
    rows = kv_ref.shape[0]
    pages, tokens, width = pool_ref.shape

    def chip_at(c):
        return (group, 2 * c + core)

    def same_member(g):
        return (g % groups, member)

    partner = (group, 2 * x + 1 - core)
    next_group = same_member(group + 1)
    first_hop = same_member(z * Y_CHIPS + (y + 3) % Y_CHIPS)
    step_up = jnp.where(y == 2, 1, 0)
    second_hop = same_member((z + step_up) * Y_CHIPS + (y + 3) % Y_CHIPS)

    def slot(c, half):
        return kv_all.at[pl.ds((2 * c + core) * rows + half * HALF, HALF)]

    def load(index, source, target):
        return pltpu.make_async_copy(source, target, load_sems.at[index])

    loads = [
        load(0, kv_ref, kv_all.at[pl.ds(member * rows, rows)]),
        load(1, row_query_ref, all_query.at[group]),
        load(2, row_pair_ref, all_pair.at[group]),
        load(3, pool_ref, pool),
        load(4, query_ref, queries),
    ]
    for copy in loads:
        copy.start()

    barrier = pltpu.get_barrier_semaphore()
    peers = [same_member(group + hop) for hop in range(1, groups)]
    peers += [partner, chip_at((x + 1) % 4), chip_at((x + 3) % 4)]
    for peer in peers:
        pl.semaphore_signal(barrier, inc=1, device_id=peer, device_id_type=MESH)
    pl.semaphore_wait(barrier, len(peers))

    def remote(source, target, send_sem, recv_sem, device):
        return pltpu.make_async_remote_copy(
            src_ref=source,
            dst_ref=target,
            send_sem=send_sem,
            recv_sem=recv_sem,
            device_id=device,
            device_id_type=MESH,
        )

    def row_copy(index, hop):
        source, target = ((row_query_ref, all_query), (row_pair_ref, all_pair))[index]
        return remote(
            source,
            target.at[group],
            row_send.at[index, hop],
            row_recv.at[index, hop],
            same_member(group + hop),
        )

    for hop in range(1, groups):
        for index in range(2):
            row_copy(index, hop).start()
    metas = [
        remote(move_table_ref, near_table_ref, meta_send.at[0], meta_recv.at[0], next_group),
        remote(move_len_ref, near_len_ref, meta_send.at[1], meta_recv.at[1], next_group),
    ]
    for copy in metas:
        copy.start()

    def kv_copy(c, half, target, lane):
        return remote(
            slot(c, half), slot(c, half), kv_send.at[lane], kv_recv.at[c, half], target
        )

    def part_copy(c, half):
        return remote(
            slot(c, half), slot(c, half), part_send.at[c, half], part_recv.at[c, half], partner
        )

    loads[0].wait()

    @pl.when(x < 3)
    def _():
        for half in range(2):
            kv_copy(x, half, chip_at(x + 1), half).start()

    @pl.when(x == 0)
    def _():
        for half in range(2):
            kv_copy(x, half, chip_at(3), 2 + half).start()

    @pl.when(x == 1)
    def _():
        kv_copy(x, 1, chip_at(0), 2).start()

    for half in range(2):
        part_copy(x, half).start()

    straight = []
    for index in range(PIECES):
        count = FORWARD_PAGES // PIECES
        part = pl.ds(index * count, count)
        straight.append(
            remote(
                pool_ref.at[part],
                raw_ref.at[part],
                page_send.at[index],
                page_recv.at[index],
                next_group,
            )
        )
        straight[-1].start()
    per_piece = (pages - FORWARD_PAGES) // PIECES

    def relay_copy(step, index):
        here = pl.ds(index * per_piece, per_piece)
        final = pl.ds(FORWARD_PAGES + index * per_piece, per_piece)
        source = pool_ref.at[final] if step == 0 else relays.at[step - 1, here]
        target = raw_ref.at[final] if step == 2 else relays.at[step, here]
        return remote(
            source,
            target,
            relay_send.at[step, index],
            relay_recv.at[step, index],
            second_hop if step == 1 else first_hop,
        )

    def relay(step, index):
        relay_copy(step - 1, index).wait_recv()
        relay_copy(step, index).start()

    for index in range(PIECES):
        relay_copy(0, index).start()

    def attend_decode():
        row = jnp.int32(0)
        for i in range(groups):
            row = jnp.where(arrival_ref[i] == group, i, row)
        flat = all_query[row].astype(jnp.float32)
        query = jnp.concatenate(
            [flat[:, g * HEAD_SIZE : (g + 1) * HEAD_SIZE] for g in range(GROUP_EXTENT)]
            + [jnp.zeros((8 - GROUP_EXTENT, HEAD_SIZE), jnp.float32)],
            axis=0,
        )
        pair = all_pair[row].astype(jnp.float32)
        cached = pool[...].reshape(pages * tokens, width)
        scores = exact_dot(
            query.astype(jnp.bfloat16), cached[:, :HEAD_SIZE], ((1,), (1,))
        )
        spot = lax.broadcasted_iota(jnp.int32, scores.shape, 1)
        page = lax.shift_right_logical(spot, 7)
        token = lax.bitwise_and(spot, tokens - 1)
        first_spot = jnp.zeros_like(spot)
        for i in range(pages):
            first_spot = jnp.where(page == table_ref[0, i], i * tokens, first_spot)
        scores = jnp.where(first_spot + token < len_ref[0], scores, NEG_FILL)
        new_score = jnp.sum(query * pair[:, :HEAD_SIZE], axis=1, keepdims=True)
        top = jnp.maximum(jnp.max(scores, axis=1, keepdims=True), new_score)
        weights = jnp.exp((scores - top) * SCALE).astype(jnp.bfloat16)
        new_weight = jnp.exp((new_score - top) * SCALE).astype(jnp.bfloat16).astype(jnp.float32)
        value = jnp.concatenate(
            [cached[:, HEAD_SIZE:], jnp.ones((pages * tokens, HEAD_SIZE), jnp.bfloat16)], axis=1
        )
        summed = exact_dot(weights, value, ((1,), (0,)))
        normed = (summed[:, :HEAD_SIZE] + new_weight * pair[:, HEAD_SIZE:]) / (
            summed[:, HEAD_SIZE:] + new_weight
        )
        for g in range(GROUP_EXTENT):
            decode_out[:, g * HEAD_SIZE : (g + 1) * HEAD_SIZE] = normed[g : g + 1].astype(
                jnp.bfloat16
            )

    for copy in loads[1:4]:
        copy.wait()
    for hop in range(1, groups):
        for index in range(2):
            row_copy(index, hop).wait()
    attend_decode()
    decode_store = pltpu.make_async_copy(decode_out, decode_ref, out_sems.at[KV_HEAD_COUNT])
    decode_store.start()

    def arrived(c, half):
        kv_copy(c, half, partner, 0).wait_recv()

    def take(c, half):
        arrived(c, half)
        part_copy(c, half).start()

    relay(1, 0)

    @pl.when(x == 1)
    def _():
        take(0, 0)

    @pl.when(x == 2)
    def _():
        arrived(1, 0)
        kv_copy(1, 0, chip_at(3), 2).start()
        part_copy(1, 0).start()

    @pl.when(x == 3)
    def _():
        arrived(0, 0)
        kv_copy(0, 0, chip_at(2), 0).start()
        part_copy(0, 0).start()
        take(2, 0)

    @pl.when(x == 0)
    def _():
        arrived(1, 1)
        kv_copy(1, 1, chip_at(3), 4).start()

    relay(1, 1)

    @pl.when(x == 1)
    def _():
        take(0, 1)

    @pl.when(x == 2)
    def _():
        take(1, 1)
        take(0, 0)

    @pl.when(x == 3)
    def _():
        arrived(0, 1)
        kv_copy(0, 1, chip_at(2), 1).start()
        part_copy(0, 1).start()
        take(2, 1)

    @pl.when(x == 2)
    def _():
        take(0, 1)

    @pl.when(x == 3)
    def _():
        take(1, 0)
        take(1, 1)

    relay(2, 0)
    for c in range(4):

        @pl.when(c <= x)
        def _():
            for half in range(2):
                part_copy(c, half).wait()

    loads[4].wait()

    def out_copy(n):
        columns = pl.ds(
            pl.multiple_of(n * GROUP_EXTENT * HEAD_SIZE, HEAD_SIZE), GROUP_EXTENT * HEAD_SIZE
        )
        return pltpu.make_async_copy(
            outs.at[:, columns], prefill_ref.at[:, columns], out_sems.at[n]
        )

    def attend(chips, n):
        keys = 256 * chips
        start = pl.multiple_of(n * 2 * HEAD_SIZE, HEAD_SIZE)
        key = kv_all[:keys, pl.ds(start, HEAD_SIZE)]
        value = jnp.concatenate(
            [
                kv_all[:keys, pl.ds(pl.multiple_of(start + HEAD_SIZE, HEAD_SIZE), HEAD_SIZE)],
                jnp.ones((keys, HEAD_SIZE), jnp.bfloat16),
            ],
            axis=1,
        )
        allowed = lax.broadcasted_iota(jnp.int32, (rows, 256), 1) <= (
            core * rows + lax.broadcasted_iota(jnp.int32, (rows, 256), 0)
        )
        for g in range(GROUP_EXTENT):
            columns = pl.ds(
                pl.multiple_of((n * GROUP_EXTENT + g) * HEAD_SIZE, HEAD_SIZE), HEAD_SIZE
            )
            scores = exact_dot(queries[:, columns], key, ((1,), (1,)))
            last = jnp.where(allowed, scores[:, keys - 256 :], NEG_FILL)
            if chips > 1:
                scores = jnp.concatenate([scores[:, : keys - 256], last], axis=1)
            else:
                scores = last
            top = jnp.max(scores, axis=1, keepdims=True)
            weights = jnp.exp((scores - top) * SCALE).astype(jnp.bfloat16)
            summed = exact_dot(weights, value, ((1,), (0,)))
            outs[:, columns] = (summed[:, :HEAD_SIZE] / summed[:, HEAD_SIZE:]).astype(
                jnp.bfloat16
            )

    def attend_head(n, carry):
        for chips in range(1, 5):
            pl.when(x == chips - 1)(functools.partial(attend, chips, n))
        out_copy(n).start()
        return carry

    middle = KV_HEAD_COUNT // 2
    lax.fori_loop(0, middle, attend_head, 0)
    relay(2, 1)
    lax.fori_loop(middle, KV_HEAD_COUNT, attend_head, 0)

    @pl.when(x == 0)
    def _():
        for lane in range(5):
            kv_copy(x, 0, chip_at(1), lane).wait_send()

    @pl.when((x == 1) | (x == 2))
    def _():
        for lane in range(3):
            kv_copy(x, 0, chip_at(3), lane).wait_send()

    @pl.when(x == 3)
    def _():
        for lane in range(2):
            kv_copy(x, 0, chip_at(2), lane).wait_send()

    decode_store.wait()

    def out_wait(n, carry):
        out_copy(n).wait()
        return carry

    lax.fori_loop(0, KV_HEAD_COUNT, out_wait, 0)
    for copy in metas:
        copy.wait()
    for index in range(PIECES):
        for step in range(3):
            relay_copy(step, index).wait_send()
        relay_copy(2, index).wait_recv()
    for copy in straight:
        copy.wait()


def attention_and_moves(
    arrival, table, lens, query, kv, row_query, row_pair, pool, move_table, move_len
):
    any_space = pl.BlockSpec(memory_space=pl.ANY)
    smem = pl.BlockSpec(memory_space=pltpu.SMEM)
    dma = pltpu.SemaphoreType.DMA
    groups = Y_CHIPS * Z_CHIPS
    pages = pool.shape[0]
    return pl.pallas_call(
        main_kernel,
        out_shape=(
            jax.ShapeDtypeStruct(query.shape, query.dtype),
            jax.ShapeDtypeStruct(row_query.shape, row_query.dtype),
            jax.ShapeDtypeStruct(pool.shape, pool.dtype),
            jax.ShapeDtypeStruct(move_table.shape, move_table.dtype),
            jax.ShapeDtypeStruct(move_len.shape, move_len.dtype),
        ),
        in_specs=[smem] * 3 + [any_space] * 7,
        out_specs=(any_space,) * 5,
        scratch_shapes=[
            pltpu.VMEM(query.shape, query.dtype),
            pltpu.VMEM((8 * kv.shape[0], kv.shape[1]), kv.dtype),
            pltpu.VMEM(pool.shape, pool.dtype),
            pltpu.VMEM(query.shape, query.dtype),
            pltpu.VMEM((groups,) + row_query.shape, row_query.dtype),
            pltpu.VMEM((groups,) + row_pair.shape, row_pair.dtype),
            pltpu.VMEM(row_query.shape, row_query.dtype),
            pltpu.VMEM((2, pages - FORWARD_PAGES) + pool.shape[1:], pool.dtype),
            dma((5,)),
            dma((KV_HEAD_COUNT + 1,)),
            dma((4, 2)),
            dma((5,)),
            dma((4, 2)),
            dma((4, 2)),
            dma((2, groups)),
            dma((2, groups)),
            dma((2,)),
            dma((2,)),
            dma((PIECES,)),
            dma((PIECES,)),
            dma((3, PIECES)),
            dma((3, PIECES)),
        ],
        compiler_params=pltpu.CompilerParams(collective_id=0, has_side_effects=True),
        name="attention_and_moves",
    )(arrival, table, lens, query, kv, row_query, row_pair, pool, move_table, move_len)


LOAD_PARTS = 4


def place_kernel(
    table_ref,
    len_ref,
    raw_ref,
    prefill_in,
    decode_in,
    out_ref,
    prefill_out,
    decode_out,
    table,
    lens,
    held,
    zero,
    passed,
    passed_row,
    in_sems,
    out_sems,
    meta_sems,
    pass_sems,
):
    pages, tokens = raw_ref.shape[0], raw_ref.shape[1]
    metas = [
        pltpu.make_async_copy(table_ref, table, meta_sems.at[0]),
        pltpu.make_async_copy(len_ref, lens, meta_sems.at[1]),
    ]
    for copy in metas:
        copy.start()
    count = pages // LOAD_PARTS
    parts = []
    for index in range(LOAD_PARTS):
        part = pl.ds(index * count, count)
        parts.append(
            pltpu.make_async_copy(raw_ref.at[part], held.at[part], in_sems.at[index])
        )
        parts[-1].start()
    into = [
        pltpu.make_async_copy(prefill_in, passed, pass_sems.at[0]),
        pltpu.make_async_copy(decode_in, passed_row, pass_sems.at[1]),
    ]
    back = [
        pltpu.make_async_copy(passed, prefill_out, pass_sems.at[2]),
        pltpu.make_async_copy(passed_row, decode_out, pass_sems.at[3]),
    ]
    for copy in into:
        copy.start()
    zero[...] = jnp.zeros_like(zero)
    for copy in metas + parts:
        copy.wait()
    for i in range(pages):
        live = i * tokens < lens[0]

        @pl.when(live)
        def _():
            pltpu.make_async_copy(held.at[table[0, i]], out_ref.at[i], out_sems.at[i]).start()

        @pl.when(jnp.logical_not(live))
        def _():
            pltpu.make_async_copy(zero, out_ref.at[i], out_sems.at[i]).start()

    for first, second in zip(into, back):
        first.wait()
        second.start()
    for i in range(pages):
        pltpu.make_async_copy(zero, out_ref.at[i], out_sems.at[i]).wait()
    for copy in back:
        copy.wait()


def place(table, lens, raw, prefill_rows, decode_rows):
    pages = raw.shape[0]
    any_space = pl.BlockSpec(memory_space=pl.ANY)
    dma = pltpu.SemaphoreType.DMA
    return pl.pallas_call(
        place_kernel,
        out_shape=tuple(
            jax.ShapeDtypeStruct(part.shape, part.dtype)
            for part in (raw, prefill_rows, decode_rows)
        ),
        in_specs=[any_space] * 5,
        out_specs=(any_space,) * 3,
        scratch_shapes=[
            pltpu.SMEM(table.shape, table.dtype),
            pltpu.SMEM(lens.shape, lens.dtype),
            pltpu.VMEM(raw.shape, raw.dtype),
            pltpu.VMEM(raw.shape[1:], raw.dtype),
            pltpu.VMEM(prefill_rows.shape, prefill_rows.dtype),
            pltpu.VMEM(decode_rows.shape, decode_rows.dtype),
            dma((LOAD_PARTS,)),
            dma((pages,)),
            dma((2,)),
            dma((4,)),
        ],
        name="place",
    )(table, lens, raw, prefill_rows, decode_rows)


def on_device(
    prefill_queries,
    prefill_key_values,
    decode_queries,
    decode_key_values,
    arrival,
    pooled_key_values,
    page_table,
    cache_len,
    mover,
):
    moving_table = lax.dynamic_slice_in_dim(page_table, mover[0], 1, 0)
    moving_len = lax.dynamic_slice_in_dim(cache_len, mover[0], 1, 0)
    prefill_rows, decode_rows, raw, near_table, near_len = attention_and_moves(
        arrival,
        page_table,
        cache_len,
        prefill_queries,
        prefill_key_values,
        decode_queries,
        decode_key_values,
        pooled_key_values,
        moving_table,
        moving_len,
    )
    received_pages, prefill_out, decode_out = place(
        near_table, near_len, raw, prefill_rows, decode_rows
    )
    return (prefill_out, decode_out, received_pages)


def solution(mesh):
    placed = (
        P(("dp", "seq"), None),
        P(("dp", "seq"), None),
        P("dp", "seq"),
        P("dp", "seq"),
        P(),
        P("dp", None, "seq"),
        P("dp", None),
        P("dp"),
        P("dp"),
    )
    return jax.shard_map(
        on_device,
        mesh=mesh,
        in_specs=placed,
        out_specs=(P(("dp", "seq"), None), P("dp", "seq"), P("dp", None, "seq")),
        check_vma=False,
    )
```

```python
import functools
import math

import jax
import jax.numpy as jnp
from jax import lax
from jax.experimental import pallas as pl
from jax.experimental.pallas import tpu as pltpu
from jax.sharding import PartitionSpec as P

QUERY_HEADS = 32
KV_HEAD_COUNT = 8
HEAD_SIZE = 128
GROUP_EXTENT = QUERY_HEADS // KV_HEAD_COUNT
NEG_FILL = -1e30
SCALE = 1.0 / math.sqrt(HEAD_SIZE)
MESH = pl.DeviceIdType.MESH
Y_CHIPS = 4
Z_CHIPS = 8
HALF = 64
FORWARD_PAGES = 24
PIECES = 4
FIRST_PAGES = 2


def exact_dot(left, right, dimensions):
    return lax.dot_general(
        left, right, (dimensions, ((), ())), preferred_element_type=jnp.float32
    )


def main_kernel(
    arrival_ref,
    table_ref,
    len_ref,
    query_ref,
    kv_ref,
    row_query_ref,
    row_pair_ref,
    pool_ref,
    move_table_ref,
    move_len_ref,
    prefill_ref,
    decode_ref,
    raw_ref,
    near_table_ref,
    near_len_ref,
    queries,
    kv_all,
    pool,
    outs,
    all_query,
    all_pair,
    decode_out,
    relays,
    load_sems,
    out_sems,
    kv_recv,
    kv_send,
    part_recv,
    part_send,
    row_recv,
    row_send,
    meta_recv,
    meta_send,
    page_recv,
    page_send,
    relay_recv,
    relay_send,
    up_recv,
    up_send,
):
    group = lax.axis_index("dp")
    member = lax.axis_index("seq")
    z, y = group // Y_CHIPS, group % Y_CHIPS
    x, core = member // 2, member % 2
    groups = Y_CHIPS * Z_CHIPS
    rows = kv_ref.shape[0]
    pages, tokens, width = pool_ref.shape

    def chip_at(c):
        return (group, 2 * c + core)

    def same_member(g):
        return (g % groups, member)

    partner = (group, 2 * x + 1 - core)
    next_group = same_member(group + 1)
    hop_down = same_member(z * Y_CHIPS + (y + 3) % Y_CHIPS)
    hop_up = same_member(group + Y_CHIPS)

    def slot(c, half):
        return kv_all.at[pl.ds((2 * c + core) * rows + half * HALF, HALF)]

    def load(index, source, target):
        return pltpu.make_async_copy(source, target, load_sems.at[index])

    loads = [
        load(0, kv_ref, kv_all.at[pl.ds(member * rows, rows)]),
        load(1, row_query_ref, all_query.at[group]),
        load(2, row_pair_ref, all_pair.at[group]),
        load(3, pool_ref, pool),
        load(4, query_ref, queries),
    ]
    for copy in loads:
        copy.start()

    barrier = pltpu.get_barrier_semaphore()
    peers = [same_member(group + hop) for hop in range(1, groups)]
    peers += [partner, chip_at((x + 1) % 4), chip_at((x + 3) % 4)]
    for peer in peers:
        pl.semaphore_signal(barrier, inc=1, device_id=peer, device_id_type=MESH)
    pl.semaphore_wait(barrier, len(peers))

    def remote(source, target, send_sem, recv_sem, device):
        return pltpu.make_async_remote_copy(
            src_ref=source,
            dst_ref=target,
            send_sem=send_sem,
            recv_sem=recv_sem,
            device_id=device,
            device_id_type=MESH,
        )

    def straight_copy(index):
        part = (pl.ds(0, FIRST_PAGES), pl.ds(FIRST_PAGES, FORWARD_PAGES - FIRST_PAGES))[index]
        return remote(
            pool_ref.at[part],
            raw_ref.at[part],
            page_send.at[index],
            page_recv.at[index],
            next_group,
        )

    per_piece = (pages - FORWARD_PAGES) // PIECES

    def relay_copy(step, index):
        here = pl.ds(index * per_piece, per_piece)
        final = pl.ds(FORWARD_PAGES + index * per_piece, per_piece)
        source = pool_ref.at[final] if step == 0 else relays.at[step - 1, here]
        target = raw_ref.at[final] if step == 2 else relays.at[step, here]
        return remote(
            source,
            target,
            relay_send.at[step, index],
            relay_recv.at[step, index],
            hop_down,
        )

    def up_copy(index):
        here = pl.ds(index * per_piece, per_piece)
        return remote(
            relays.at[0, here], relays.at[2, here], up_send.at[index], up_recv.at[index], hop_up
        )

    def raised_copy(index):
        here = pl.ds(index * per_piece, per_piece)
        return remote(
            relays.at[2, here],
            relays.at[1, here],
            relay_send.at[1, index],
            relay_recv.at[1, index],
            hop_down,
        )

    def first_relay(index):
        relay_copy(0, index).wait_recv()

        @pl.when(y == 2)
        def _():
            up_copy(index).start()

        @pl.when(y != 2)
        def _():
            relay_copy(1, index).start()

    def raised_relay(index):
        @pl.when(y == 2)
        def _():
            up_copy(index).wait_recv()
            raised_copy(index).start()

    def last_relay(index):
        relay_copy(1, index).wait_recv()
        relay_copy(2, index).start()

    straight_copy(0).start()
    relay_copy(0, 0).start()

    def row_copy(index, hop):
        source, target = ((row_query_ref, all_query), (row_pair_ref, all_pair))[index]
        return remote(
            source,
            target.at[group],
            row_send.at[index, hop],
            row_recv.at[index, hop],
            same_member(group + hop),
        )

    def kv_copy(c, half, target, lane):
        return remote(
            slot(c, half), slot(c, half), kv_send.at[lane], kv_recv.at[c, half], target
        )

    def part_copy(c, half):
        return remote(
            slot(c, half), slot(c, half), part_send.at[c, half], part_recv.at[c, half], partner
        )

    loads[0].wait()

    @pl.when(x < 3)
    def _():
        for half in range(2):
            kv_copy(x, half, chip_at(x + 1), half).start()

    @pl.when(x == 0)
    def _():
        for half in range(2):
            kv_copy(x, half, chip_at(3), 2 + half).start()

    @pl.when(x == 1)
    def _():
        kv_copy(x, 1, chip_at(0), 2).start()

    for half in range(2):
        part_copy(x, half).start()

    for hop in range(1, groups):
        for index in range(2):
            row_copy(index, hop).start()
    metas = [
        remote(move_table_ref, near_table_ref, meta_send.at[0], meta_recv.at[0], next_group),
        remote(move_len_ref, near_len_ref, meta_send.at[1], meta_recv.at[1], next_group),
    ]
    for copy in metas:
        copy.start()

    straight_copy(1).start()
    for index in range(1, PIECES):
        relay_copy(0, index).start()

    def attend_decode():
        row = jnp.int32(0)
        for i in range(groups):
            row = jnp.where(arrival_ref[i] == group, i, row)
        flat = all_query[row].astype(jnp.float32)
        query = jnp.concatenate(
            [flat[:, g * HEAD_SIZE : (g + 1) * HEAD_SIZE] for g in range(GROUP_EXTENT)]
            + [jnp.zeros((8 - GROUP_EXTENT, HEAD_SIZE), jnp.float32)],
            axis=0,
        )
        pair = all_pair[row].astype(jnp.float32)
        cached = pool[...].reshape(pages * tokens, width)
        scores = exact_dot(
            query.astype(jnp.bfloat16), cached[:, :HEAD_SIZE], ((1,), (1,))
        )
        spot = lax.broadcasted_iota(jnp.int32, scores.shape, 1)
        page = lax.shift_right_logical(spot, 7)
        token = lax.bitwise_and(spot, tokens - 1)
        first_spot = jnp.zeros_like(spot)
        for i in range(pages):
            first_spot = jnp.where(page == table_ref[0, i], i * tokens, first_spot)
        scores = jnp.where(first_spot + token < len_ref[0], scores, NEG_FILL)
        new_score = jnp.sum(query * pair[:, :HEAD_SIZE], axis=1, keepdims=True)
        top = jnp.maximum(jnp.max(scores, axis=1, keepdims=True), new_score)
        weights = jnp.exp((scores - top) * SCALE).astype(jnp.bfloat16)
        new_weight = jnp.exp((new_score - top) * SCALE).astype(jnp.bfloat16).astype(jnp.float32)
        value = jnp.concatenate(
            [cached[:, HEAD_SIZE:], jnp.ones((pages * tokens, HEAD_SIZE), jnp.bfloat16)], axis=1
        )
        summed = exact_dot(weights, value, ((1,), (0,)))
        normed = (summed[:, :HEAD_SIZE] + new_weight * pair[:, HEAD_SIZE:]) / (
            summed[:, HEAD_SIZE:] + new_weight
        )
        for g in range(GROUP_EXTENT):
            decode_out[:, g * HEAD_SIZE : (g + 1) * HEAD_SIZE] = normed[g : g + 1].astype(
                jnp.bfloat16
            )

    def arrived(c, half):
        kv_copy(c, half, partner, 0).wait_recv()

    def take(c, half):
        arrived(c, half)
        part_copy(c, half).start()

    first_relay(0)
    first_relay(1)

    @pl.when(x == 1)
    def _():
        take(0, 0)

    @pl.when(x == 2)
    def _():
        arrived(1, 0)
        kv_copy(1, 0, chip_at(3), 2).start()
        part_copy(1, 0).start()

    @pl.when(x == 3)
    def _():
        arrived(0, 0)
        kv_copy(0, 0, chip_at(2), 0).start()
        part_copy(0, 0).start()
        take(2, 0)

    @pl.when(x == 0)
    def _():
        arrived(1, 1)
        kv_copy(1, 1, chip_at(3), 4).start()

    raised_relay(0)
    first_relay(2)
    raised_relay(1)
    first_relay(3)

    @pl.when(x == 1)
    def _():
        take(0, 1)

    @pl.when(x == 2)
    def _():
        take(1, 1)

    @pl.when(x == 3)
    def _():
        arrived(0, 1)
        kv_copy(0, 1, chip_at(2), 1).start()
        part_copy(0, 1).start()
        take(2, 1)

    for copy in loads[1:4]:
        copy.wait()
    for hop in range(1, groups):
        for index in range(2):
            row_copy(index, hop).wait()
    attend_decode()
    decode_store = pltpu.make_async_copy(decode_out, decode_ref, out_sems.at[KV_HEAD_COUNT])
    decode_store.start()

    raised_relay(2)
    last_relay(0)
    raised_relay(3)

    @pl.when(x == 2)
    def _():
        take(0, 0)
        take(0, 1)

    @pl.when(x == 3)
    def _():
        take(1, 0)
        take(1, 1)

    last_relay(1)
    for c in range(4):

        @pl.when(c <= x)
        def _():
            for half in range(2):
                part_copy(c, half).wait()

    loads[4].wait()

    def out_copy(n):
        columns = pl.ds(
            pl.multiple_of(n * GROUP_EXTENT * HEAD_SIZE, HEAD_SIZE), GROUP_EXTENT * HEAD_SIZE
        )
        return pltpu.make_async_copy(
            outs.at[:, columns], prefill_ref.at[:, columns], out_sems.at[n]
        )

    def attend(chips, n):
        keys = 256 * chips
        start = pl.multiple_of(n * 2 * HEAD_SIZE, HEAD_SIZE)
        key = kv_all[:keys, pl.ds(start, HEAD_SIZE)]
        value = jnp.concatenate(
            [
                kv_all[:keys, pl.ds(pl.multiple_of(start + HEAD_SIZE, HEAD_SIZE), HEAD_SIZE)],
                jnp.ones((keys, HEAD_SIZE), jnp.bfloat16),
            ],
            axis=1,
        )
        allowed = lax.broadcasted_iota(jnp.int32, (rows, 256), 1) <= (
            core * rows + lax.broadcasted_iota(jnp.int32, (rows, 256), 0)
        )
        for g in range(GROUP_EXTENT):
            columns = pl.ds(
                pl.multiple_of((n * GROUP_EXTENT + g) * HEAD_SIZE, HEAD_SIZE), HEAD_SIZE
            )
            scores = exact_dot(queries[:, columns], key, ((1,), (1,)))
            last = jnp.where(allowed, scores[:, keys - 256 :], NEG_FILL)
            if chips > 1:
                scores = jnp.concatenate([scores[:, : keys - 256], last], axis=1)
            else:
                scores = last
            top = jnp.max(scores, axis=1, keepdims=True)
            weights = jnp.exp((scores - top) * SCALE).astype(jnp.bfloat16)
            summed = exact_dot(weights, value, ((1,), (0,)))
            outs[:, columns] = (summed[:, :HEAD_SIZE] / summed[:, HEAD_SIZE:]).astype(
                jnp.bfloat16
            )

    def attend_head(n, carry):
        for chips in range(1, 5):
            pl.when(x == chips - 1)(functools.partial(attend, chips, n))
        out_copy(n).start()
        return carry

    def attend_then_relay(n, carry):
        attend_head(n, carry)
        pl.when(n == 1)(functools.partial(last_relay, 2))
        pl.when(n == 3)(functools.partial(last_relay, 3))
        return carry

    lax.fori_loop(0, KV_HEAD_COUNT, attend_then_relay, 0)

    @pl.when(x == 0)
    def _():
        for lane in range(5):
            kv_copy(x, 0, chip_at(1), lane).wait_send()

    @pl.when((x == 1) | (x == 2))
    def _():
        for lane in range(3):
            kv_copy(x, 0, chip_at(3), lane).wait_send()

    @pl.when(x == 3)
    def _():
        for lane in range(2):
            kv_copy(x, 0, chip_at(2), lane).wait_send()

    decode_store.wait()

    def out_wait(n, carry):
        out_copy(n).wait()
        return carry

    lax.fori_loop(0, KV_HEAD_COUNT, out_wait, 0)
    for copy in metas:
        copy.wait()
    for index in range(PIECES):
        for step in range(3):
            relay_copy(step, index).wait_send()

        @pl.when(y == 2)
        def _():
            up_copy(index).wait_send()

        relay_copy(2, index).wait_recv()
    for index in range(2):
        straight_copy(index).wait()


def attention_and_moves(
    arrival, table, lens, query, kv, row_query, row_pair, pool, move_table, move_len
):
    any_space = pl.BlockSpec(memory_space=pl.ANY)
    smem = pl.BlockSpec(memory_space=pltpu.SMEM)
    dma = pltpu.SemaphoreType.DMA
    groups = Y_CHIPS * Z_CHIPS
    pages = pool.shape[0]
    return pl.pallas_call(
        main_kernel,
        out_shape=(
            jax.ShapeDtypeStruct(query.shape, query.dtype),
            jax.ShapeDtypeStruct(row_query.shape, row_query.dtype),
            jax.ShapeDtypeStruct(pool.shape, pool.dtype),
            jax.ShapeDtypeStruct(move_table.shape, move_table.dtype),
            jax.ShapeDtypeStruct(move_len.shape, move_len.dtype),
        ),
        in_specs=[smem] * 3 + [any_space] * 7,
        out_specs=(any_space,) * 5,
        scratch_shapes=[
            pltpu.VMEM(query.shape, query.dtype),
            pltpu.VMEM((8 * kv.shape[0], kv.shape[1]), kv.dtype),
            pltpu.VMEM(pool.shape, pool.dtype),
            pltpu.VMEM(query.shape, query.dtype),
            pltpu.VMEM((groups,) + row_query.shape, row_query.dtype),
            pltpu.VMEM((groups,) + row_pair.shape, row_pair.dtype),
            pltpu.VMEM(row_query.shape, row_query.dtype),
            pltpu.VMEM((3, pages - FORWARD_PAGES) + pool.shape[1:], pool.dtype),
            dma((5,)),
            dma((KV_HEAD_COUNT + 1,)),
            dma((4, 2)),
            dma((5,)),
            dma((4, 2)),
            dma((4, 2)),
            dma((2, groups)),
            dma((2, groups)),
            dma((2,)),
            dma((2,)),
            dma((2,)),
            dma((2,)),
            dma((3, PIECES)),
            dma((3, PIECES)),
            dma((PIECES,)),
            dma((PIECES,)),
        ],
        compiler_params=pltpu.CompilerParams(
            collective_id=0, has_side_effects=True, vmem_limit_bytes=28 << 20
        ),
        name="attention_and_moves",
    )(
        arrival,
        table,
        lens,
        *(
            pltpu.with_memory_space_constraint(part, pltpu.HBM)
            for part in (query, kv, row_query, row_pair, pool)
        ),
        move_table,
        move_len,
    )


def place_kernel(
    table_ref,
    len_ref,
    raw_ref,
    prefill_in,
    decode_in,
    out_ref,
    prefill_out,
    decode_out,
    table,
    lens,
    zero,
    out_sems,
    meta_sems,
    pass_sems,
):
    pages, tokens = raw_ref.shape[0], raw_ref.shape[1]
    metas = [
        pltpu.make_async_copy(table_ref, table, meta_sems.at[0]),
        pltpu.make_async_copy(len_ref, lens, meta_sems.at[1]),
    ]
    passed = [
        pltpu.make_async_copy(prefill_in, prefill_out, pass_sems.at[0]),
        pltpu.make_async_copy(decode_in, decode_out, pass_sems.at[1]),
    ]
    for copy in metas + passed:
        copy.start()
    zero[...] = jnp.zeros_like(zero)
    for copy in metas:
        copy.wait()
    for i in range(pages):
        live = i * tokens < lens[0]

        @pl.when(live)
        def _():
            pltpu.make_async_copy(
                raw_ref.at[table[0, i]], out_ref.at[i], out_sems.at[i]
            ).start()

        @pl.when(jnp.logical_not(live))
        def _():
            pltpu.make_async_copy(zero, out_ref.at[i], out_sems.at[i]).start()

    for i in range(pages):
        pltpu.make_async_copy(zero, out_ref.at[i], out_sems.at[i]).wait()
    for copy in passed:
        copy.wait()


def place(table, lens, raw, prefill_rows, decode_rows):
    pages = raw.shape[0]
    any_space = pl.BlockSpec(memory_space=pl.ANY)
    dma = pltpu.SemaphoreType.DMA
    return pl.pallas_call(
        place_kernel,
        out_shape=tuple(
            jax.ShapeDtypeStruct(part.shape, part.dtype)
            for part in (raw, prefill_rows, decode_rows)
        ),
        in_specs=[any_space] * 5,
        out_specs=(any_space,) * 3,
        scratch_shapes=[
            pltpu.SMEM(table.shape, table.dtype),
            pltpu.SMEM(lens.shape, lens.dtype),
            pltpu.VMEM(raw.shape[1:], raw.dtype),
            dma((pages,)),
            dma((2,)),
            dma((2,)),
        ],
        compiler_params=pltpu.CompilerParams(vmem_limit_bytes=8 << 20),
        name="place",
    )(table, lens, raw, prefill_rows, decode_rows)


def on_device(
    prefill_queries,
    prefill_key_values,
    decode_queries,
    decode_key_values,
    arrival,
    pooled_key_values,
    page_table,
    cache_len,
    mover,
):
    moving_table = lax.dynamic_slice_in_dim(page_table, mover[0], 1, 0)
    moving_len = lax.dynamic_slice_in_dim(cache_len, mover[0], 1, 0)
    prefill_rows, decode_rows, raw, near_table, near_len = attention_and_moves(
        arrival,
        page_table,
        cache_len,
        prefill_queries,
        prefill_key_values,
        decode_queries,
        decode_key_values,
        pooled_key_values,
        moving_table,
        moving_len,
    )
    received_pages, prefill_out, decode_out = place(
        near_table, near_len, raw, prefill_rows, decode_rows
    )
    return (prefill_out, decode_out, received_pages)


def solution(mesh):
    placed = (
        P(("dp", "seq"), None),
        P(("dp", "seq"), None),
        P("dp", "seq"),
        P("dp", "seq"),
        P(),
        P("dp", None, "seq"),
        P("dp", None),
        P("dp"),
        P("dp"),
    )
    return jax.shard_map(
        on_device,
        mesh=mesh,
        in_specs=placed,
        out_specs=(P(("dp", "seq"), None), P("dp", "seq"), P("dp", None, "seq")),
        check_vma=False,
    )
```

```python
import functools
import math

import jax
import jax.numpy as jnp
from jax import lax
from jax.experimental import pallas as pl
from jax.experimental.pallas import tpu as pltpu
from jax.sharding import PartitionSpec as P

QUERY_HEADS = 32
KV_HEAD_COUNT = 8
HEAD_SIZE = 128
GROUP_EXTENT = QUERY_HEADS // KV_HEAD_COUNT
NEG_FILL = -1e30
SCALE = 1.0 / math.sqrt(HEAD_SIZE)
MESH = pl.DeviceIdType.MESH
Y_CHIPS = 4
Z_CHIPS = 8
HALF = 64
FORWARD_PAGES = 24
PIECES = 4
FIRST_PAGES = 2


def exact_dot(left, right, dimensions):
    return lax.dot_general(
        left, right, (dimensions, ((), ())), preferred_element_type=jnp.float32
    )


def main_kernel(
    arrival_in,
    table_in,
    len_ref,
    query_ref,
    kv_ref,
    row_query_ref,
    row_pair_ref,
    pool_ref,
    move_table_ref,
    move_len_ref,
    prefill_ref,
    decode_ref,
    raw_ref,
    near_table_ref,
    near_len_ref,
    queries,
    kv_all,
    pool,
    outs,
    all_query,
    all_pair,
    decode_out,
    relays,
    arrival_ref,
    table_ref,
    load_sems,
    out_sems,
    kv_recv,
    kv_send,
    part_recv,
    part_send,
    row_recv,
    row_send,
    round_recv,
    round_send,
    meta_recv,
    meta_send,
    page_recv,
    page_send,
    relay_recv,
    relay_send,
    up_recv,
    up_send,
):
    group = lax.axis_index("dp")
    member = lax.axis_index("seq")
    z, y = group // Y_CHIPS, group % Y_CHIPS
    x, core = member // 2, member % 2
    groups = Y_CHIPS * Z_CHIPS
    rows = kv_ref.shape[0]
    pages, tokens, width = pool_ref.shape

    def chip_at(c):
        return (group, 2 * c + core)

    def same_member(g):
        return ((g + groups) % groups, member)

    partner = (group, 2 * x + 1 - core)
    next_group = same_member(group + 1)
    hop_down = same_member(z * Y_CHIPS + (y + 3) % Y_CHIPS)
    hop_up = same_member(group + Y_CHIPS)

    def slot(c, half):
        return kv_all.at[pl.ds((2 * c + core) * rows + half * HALF, HALF)]

    def load(index, source, target):
        return pltpu.make_async_copy(source, target, load_sems.at[index])

    loads = [
        load(0, kv_ref, kv_all.at[pl.ds(member * rows, rows)]),
        load(1, row_query_ref, all_query.at[group]),
        load(2, row_pair_ref, all_pair.at[group]),
        load(3, pool_ref, pool),
        load(4, query_ref, queries),
        load(5, arrival_in, arrival_ref),
        load(6, table_in, table_ref),
    ]
    for copy in loads:
        copy.start()

    barrier = pltpu.get_barrier_semaphore()
    peers = [partner, chip_at((x + 1) % 4), chip_at((x + 3) % 4)]
    peers += [same_member(z * Y_CHIPS + (y + hop) % Y_CHIPS) for hop in range(1, Y_CHIPS)]
    peers += [same_member(group + hop) for hop in (1, -1, Y_CHIPS, -Y_CHIPS)]
    for peer in peers:
        pl.semaphore_signal(barrier, inc=1, device_id=peer, device_id_type=MESH)
    pl.semaphore_wait(barrier, len(peers))

    def remote(source, target, send_sem, recv_sem, device):
        return pltpu.make_async_remote_copy(
            src_ref=source,
            dst_ref=target,
            send_sem=send_sem,
            recv_sem=recv_sem,
            device_id=device,
            device_id_type=MESH,
        )

    def straight_copy(index):
        part = (pl.ds(0, FIRST_PAGES), pl.ds(FIRST_PAGES, FORWARD_PAGES - FIRST_PAGES))[index]
        return remote(
            pool_ref.at[part],
            raw_ref.at[part],
            page_send.at[index],
            page_recv.at[index],
            next_group,
        )

    per_piece = (pages - FORWARD_PAGES) // PIECES

    def relay_copy(step, index):
        here = pl.ds(index * per_piece, per_piece)
        final = pl.ds(FORWARD_PAGES + index * per_piece, per_piece)
        source = pool_ref.at[final] if step == 0 else relays.at[step - 1, here]
        target = raw_ref.at[final] if step == 2 else relays.at[step, here]
        return remote(
            source,
            target,
            relay_send.at[step, index],
            relay_recv.at[step, index],
            hop_down,
        )

    def up_copy(index):
        here = pl.ds(index * per_piece, per_piece)
        return remote(
            relays.at[0, here], relays.at[2, here], up_send.at[index], up_recv.at[index], hop_up
        )

    def raised_copy(index):
        here = pl.ds(index * per_piece, per_piece)
        return remote(
            relays.at[2, here],
            relays.at[1, here],
            relay_send.at[1, index],
            relay_recv.at[1, index],
            hop_down,
        )

    def first_relay(index):
        relay_copy(0, index).wait_recv()

        @pl.when(y == 2)
        def _():
            up_copy(index).start()

        @pl.when(y != 2)
        def _():
            relay_copy(1, index).start()

    def raised_relay(index):
        @pl.when(y == 2)
        def _():
            up_copy(index).wait_recv()
            raised_copy(index).start()

    def last_relay(index):
        relay_copy(1, index).wait_recv()
        relay_copy(2, index).start()

    straight_copy(0).start()
    relay_copy(0, 0).start()

    def row_copy(index, hop):
        source, target = ((row_query_ref, all_query), (row_pair_ref, all_pair))[index]
        return remote(
            source,
            target.at[group],
            row_send.at[index, hop],
            row_recv.at[index, hop],
            same_member(z * Y_CHIPS + (y + hop) % Y_CHIPS),
        )

    def round_copy(index, hop):
        first = ((z + hop) % Z_CHIPS) * Y_CHIPS
        block = (all_query, all_pair)[index].at[pl.ds(first, Y_CHIPS)]
        return remote(
            block,
            block,
            round_send.at[index, hop],
            round_recv.at[index, hop],
            same_member(group - Y_CHIPS),
        )

    def pass_rows(hop):
        for index in range(2):
            if hop == 0:
                loads[1 + index].wait()
                for other in range(1, Y_CHIPS):
                    row_copy(index, other).wait()
            else:
                round_copy(index, hop - 1).wait_recv()
            if hop < Z_CHIPS - 1:
                round_copy(index, hop).start()

    def kv_copy(c, half, target, lane):
        return remote(
            slot(c, half), slot(c, half), kv_send.at[lane], kv_recv.at[c, half], target
        )

    def part_copy(c, half):
        return remote(
            slot(c, half), slot(c, half), part_send.at[c, half], part_recv.at[c, half], partner
        )

    loads[0].wait()

    @pl.when(x < 3)
    def _():
        for half in range(2):
            kv_copy(x, half, chip_at(x + 1), half).start()

    @pl.when(x == 0)
    def _():
        for half in range(2):
            kv_copy(x, half, chip_at(3), 2 + half).start()

    @pl.when(x == 1)
    def _():
        kv_copy(x, 1, chip_at(0), 2).start()

    for half in range(2):
        part_copy(x, half).start()

    for hop in range(1, Y_CHIPS):
        for index in range(2):
            row_copy(index, hop).start()
    metas = [
        remote(move_table_ref, near_table_ref, meta_send.at[0], meta_recv.at[0], next_group),
        remote(move_len_ref, near_len_ref, meta_send.at[1], meta_recv.at[1], next_group),
    ]
    for copy in metas:
        copy.start()

    straight_copy(1).start()
    for index in range(1, PIECES):
        relay_copy(0, index).start()

    def attend_decode():
        row = jnp.int32(0)
        for i in range(groups):
            row = jnp.where(arrival_ref[i] == group, i, row)
        flat = all_query[row].astype(jnp.float32)
        query = jnp.concatenate(
            [flat[:, g * HEAD_SIZE : (g + 1) * HEAD_SIZE] for g in range(GROUP_EXTENT)]
            + [jnp.zeros((8 - GROUP_EXTENT, HEAD_SIZE), jnp.float32)],
            axis=0,
        )
        pair = all_pair[row].astype(jnp.float32)
        cached = pool[...].reshape(pages * tokens, width)
        scores = exact_dot(
            query.astype(jnp.bfloat16), cached[:, :HEAD_SIZE], ((1,), (1,))
        )
        spot = lax.broadcasted_iota(jnp.int32, scores.shape, 1)
        page = lax.shift_right_logical(spot, 7)
        token = lax.bitwise_and(spot, tokens - 1)
        first_spot = jnp.zeros_like(spot)
        for i in range(pages):
            first_spot = jnp.where(page == table_ref[0, i], i * tokens, first_spot)
        scores = jnp.where(first_spot + token < len_ref[0], scores, NEG_FILL)
        new_score = jnp.sum(query * pair[:, :HEAD_SIZE], axis=1, keepdims=True)
        top = jnp.maximum(jnp.max(scores, axis=1, keepdims=True), new_score)
        weights = jnp.exp((scores - top) * SCALE).astype(jnp.bfloat16)
        new_weight = jnp.exp((new_score - top) * SCALE).astype(jnp.bfloat16).astype(jnp.float32)
        value = jnp.concatenate(
            [cached[:, HEAD_SIZE:], jnp.ones((pages * tokens, HEAD_SIZE), jnp.bfloat16)], axis=1
        )
        summed = exact_dot(weights, value, ((1,), (0,)))
        normed = (summed[:, :HEAD_SIZE] + new_weight * pair[:, HEAD_SIZE:]) / (
            summed[:, HEAD_SIZE:] + new_weight
        )
        for g in range(GROUP_EXTENT):
            decode_out[:, g * HEAD_SIZE : (g + 1) * HEAD_SIZE] = normed[g : g + 1].astype(
                jnp.bfloat16
            )

    def arrived(c, half):
        kv_copy(c, half, partner, 0).wait_recv()

    def take(c, half):
        arrived(c, half)
        part_copy(c, half).start()

    first_relay(0)
    first_relay(1)
    pass_rows(0)

    @pl.when(x == 1)
    def _():
        take(0, 0)

    @pl.when(x == 2)
    def _():
        arrived(1, 0)
        kv_copy(1, 0, chip_at(3), 2).start()
        part_copy(1, 0).start()

    @pl.when(x == 3)
    def _():
        arrived(0, 0)
        kv_copy(0, 0, chip_at(2), 0).start()
        part_copy(0, 0).start()
        take(2, 0)

    @pl.when(x == 0)
    def _():
        arrived(1, 1)
        kv_copy(1, 1, chip_at(3), 4).start()

    first_relay(2)
    raised_relay(0)
    pass_rows(1)
    first_relay(3)
    raised_relay(1)
    pass_rows(2)

    @pl.when(x == 1)
    def _():
        take(0, 1)

    @pl.when(x == 2)
    def _():
        take(1, 1)

    @pl.when(x == 3)
    def _():
        arrived(0, 1)
        kv_copy(0, 1, chip_at(2), 1).start()
        part_copy(0, 1).start()
        take(2, 1)

    pass_rows(3)
    raised_relay(2)
    last_relay(0)
    pass_rows(4)
    raised_relay(3)

    @pl.when(x == 2)
    def _():
        take(0, 0)
        take(0, 1)

    @pl.when(x == 3)
    def _():
        take(1, 0)
        take(1, 1)

    last_relay(1)
    pass_rows(5)
    for c in range(4):

        @pl.when(c <= x)
        def _():
            for half in range(2):
                part_copy(c, half).wait()

    loads[4].wait()

    def out_copy(n):
        columns = pl.ds(
            pl.multiple_of(n * GROUP_EXTENT * HEAD_SIZE, HEAD_SIZE), GROUP_EXTENT * HEAD_SIZE
        )
        return pltpu.make_async_copy(
            outs.at[:, columns], prefill_ref.at[:, columns], out_sems.at[n]
        )

    def attend(chips, n):
        keys = 256 * chips
        start = pl.multiple_of(n * 2 * HEAD_SIZE, HEAD_SIZE)
        key = kv_all[:keys, pl.ds(start, HEAD_SIZE)]
        value = jnp.concatenate(
            [
                kv_all[:keys, pl.ds(pl.multiple_of(start + HEAD_SIZE, HEAD_SIZE), HEAD_SIZE)],
                jnp.ones((keys, HEAD_SIZE), jnp.bfloat16),
            ],
            axis=1,
        )
        allowed = lax.broadcasted_iota(jnp.int32, (rows, 256), 1) <= (
            core * rows + lax.broadcasted_iota(jnp.int32, (rows, 256), 0)
        )
        for g in range(GROUP_EXTENT):
            columns = pl.ds(
                pl.multiple_of((n * GROUP_EXTENT + g) * HEAD_SIZE, HEAD_SIZE), HEAD_SIZE
            )
            scores = exact_dot(queries[:, columns], key, ((1,), (1,)))
            last = jnp.where(allowed, scores[:, keys - 256 :], NEG_FILL)
            if chips > 1:
                scores = jnp.concatenate([scores[:, : keys - 256], last], axis=1)
            else:
                scores = last
            top = jnp.max(scores, axis=1, keepdims=True)
            weights = jnp.exp((scores - top) * SCALE).astype(jnp.bfloat16)
            summed = exact_dot(weights, value, ((1,), (0,)))
            outs[:, columns] = (summed[:, :HEAD_SIZE] / summed[:, HEAD_SIZE:]).astype(
                jnp.bfloat16
            )

    def attend_head(n, carry):
        for chips in range(1, 5):
            pl.when(x == chips - 1)(functools.partial(attend, chips, n))
        out_copy(n).start()
        return carry

    def attend_then_relay(n, carry):
        attend_head(n, carry)
        pl.when(n == 0)(functools.partial(pass_rows, 6))
        pl.when(n == 1)(functools.partial(last_relay, 2))
        pl.when(n == 3)(functools.partial(last_relay, 3))
        return carry

    lax.fori_loop(0, KV_HEAD_COUNT, attend_then_relay, 0)

    pass_rows(7)
    for index in (3, 5, 6):
        loads[index].wait()
    attend_decode()
    decode_store = pltpu.make_async_copy(decode_out, decode_ref, out_sems.at[KV_HEAD_COUNT])
    decode_store.start()

    @pl.when(x == 0)
    def _():
        for lane in range(5):
            kv_copy(x, 0, chip_at(1), lane).wait_send()

    @pl.when((x == 1) | (x == 2))
    def _():
        for lane in range(3):
            kv_copy(x, 0, chip_at(3), lane).wait_send()

    @pl.when(x == 3)
    def _():
        for lane in range(2):
            kv_copy(x, 0, chip_at(2), lane).wait_send()

    decode_store.wait()

    def out_wait(n, carry):
        out_copy(n).wait()
        return carry

    lax.fori_loop(0, KV_HEAD_COUNT, out_wait, 0)
    for copy in metas:
        copy.wait()
    for index in range(2):
        for hop in range(Z_CHIPS - 1):
            round_copy(index, hop).wait_send()
    for index in range(PIECES):
        for step in range(3):
            relay_copy(step, index).wait_send()

        @pl.when(y == 2)
        def _():
            up_copy(index).wait_send()

        relay_copy(2, index).wait_recv()
    for index in range(2):
        straight_copy(index).wait()


def in_hbm(array):
    return pltpu.with_memory_space_constraint(array, pltpu.HBM)


def attention_and_moves(
    arrival, table, lens, query, kv, row_query, row_pair, pool, move_table, move_len
):
    any_space = pl.BlockSpec(memory_space=pl.ANY)
    dma = pltpu.SemaphoreType.DMA
    groups = Y_CHIPS * Z_CHIPS
    pages = pool.shape[0]
    return pl.pallas_call(
        main_kernel,
        out_shape=(
            jax.ShapeDtypeStruct(query.shape, query.dtype),
            jax.ShapeDtypeStruct(row_query.shape, row_query.dtype),
            jax.ShapeDtypeStruct(pool.shape, pool.dtype),
            jax.ShapeDtypeStruct(move_table.shape, move_table.dtype),
            jax.ShapeDtypeStruct(move_len.shape, move_len.dtype),
        ),
        in_specs=[any_space] * 2 + [pl.BlockSpec(memory_space=pltpu.SMEM)] + [any_space] * 7,
        out_specs=(any_space,) * 5,
        scratch_shapes=[
            pltpu.VMEM(query.shape, query.dtype),
            pltpu.VMEM((8 * kv.shape[0], kv.shape[1]), kv.dtype),
            pltpu.VMEM(pool.shape, pool.dtype),
            pltpu.VMEM(query.shape, query.dtype),
            pltpu.VMEM((groups,) + row_query.shape, row_query.dtype),
            pltpu.VMEM((groups,) + row_pair.shape, row_pair.dtype),
            pltpu.VMEM(row_query.shape, row_query.dtype),
            pltpu.VMEM((3, pages - FORWARD_PAGES) + pool.shape[1:], pool.dtype),
            pltpu.SMEM(arrival.shape, arrival.dtype),
            pltpu.SMEM(table.shape, table.dtype),
            dma((7,)),
            dma((KV_HEAD_COUNT + 1,)),
            dma((4, 2)),
            dma((5,)),
            dma((4, 2)),
            dma((4, 2)),
            dma((2, Y_CHIPS)),
            dma((2, Y_CHIPS)),
            dma((2, Z_CHIPS)),
            dma((2, Z_CHIPS)),
            dma((2,)),
            dma((2,)),
            dma((2,)),
            dma((2,)),
            dma((3, PIECES)),
            dma((3, PIECES)),
            dma((PIECES,)),
            dma((PIECES,)),
        ],
        compiler_params=pltpu.CompilerParams(
            collective_id=0, has_side_effects=True, vmem_limit_bytes=28 << 20
        ),
        name="attention_and_moves",
    )(
        in_hbm(arrival),
        in_hbm(table),
        lens,
        in_hbm(query),
        in_hbm(kv),
        in_hbm(row_query),
        in_hbm(row_pair),
        in_hbm(pool),
        in_hbm(move_table),
        move_len,
    )


def place_kernel(
    table_ref,
    len_ref,
    raw_ref,
    prefill_in,
    decode_in,
    out_ref,
    prefill_out,
    decode_out,
    table,
    lens,
    zero,
    out_sems,
    meta_sems,
    pass_sems,
):
    pages, tokens = raw_ref.shape[0], raw_ref.shape[1]
    metas = [
        pltpu.make_async_copy(table_ref, table, meta_sems.at[0]),
        pltpu.make_async_copy(len_ref, lens, meta_sems.at[1]),
    ]
    passed = [
        pltpu.make_async_copy(prefill_in, prefill_out, pass_sems.at[0]),
        pltpu.make_async_copy(decode_in, decode_out, pass_sems.at[1]),
    ]
    for copy in metas + passed:
        copy.start()
    zero[...] = jnp.zeros_like(zero)
    for copy in metas:
        copy.wait()
    for i in range(pages):
        live = i * tokens < lens[0]

        @pl.when(live)
        def _():
            pltpu.make_async_copy(
                raw_ref.at[table[0, i]], out_ref.at[i], out_sems.at[i]
            ).start()

        @pl.when(jnp.logical_not(live))
        def _():
            pltpu.make_async_copy(zero, out_ref.at[i], out_sems.at[i]).start()

    for i in range(pages):
        pltpu.make_async_copy(zero, out_ref.at[i], out_sems.at[i]).wait()
    for copy in passed:
        copy.wait()


def place(table, lens, raw, prefill_rows, decode_rows):
    pages = raw.shape[0]
    any_space = pl.BlockSpec(memory_space=pl.ANY)
    dma = pltpu.SemaphoreType.DMA
    return pl.pallas_call(
        place_kernel,
        out_shape=tuple(
            jax.ShapeDtypeStruct(part.shape, part.dtype)
            for part in (raw, prefill_rows, decode_rows)
        ),
        in_specs=[any_space] * 5,
        out_specs=(any_space,) * 3,
        scratch_shapes=[
            pltpu.SMEM(table.shape, table.dtype),
            pltpu.SMEM(lens.shape, lens.dtype),
            pltpu.VMEM(raw.shape[1:], raw.dtype),
            dma((pages,)),
            dma((2,)),
            dma((2,)),
        ],
        compiler_params=pltpu.CompilerParams(vmem_limit_bytes=8 << 20),
        name="place",
    )(table, lens, raw, prefill_rows, decode_rows)


def on_device(
    prefill_queries,
    prefill_key_values,
    decode_queries,
    decode_key_values,
    arrival,
    pooled_key_values,
    page_table,
    cache_len,
    mover,
):
    moving_table = lax.dynamic_slice_in_dim(page_table, mover[0], 1, 0)
    moving_len = lax.dynamic_slice_in_dim(cache_len, mover[0], 1, 0)
    prefill_rows, decode_rows, raw, near_table, near_len = attention_and_moves(
        arrival,
        page_table,
        cache_len,
        prefill_queries,
        prefill_key_values,
        decode_queries,
        decode_key_values,
        pooled_key_values,
        moving_table,
        moving_len,
    )
    received_pages, prefill_out, decode_out = place(
        near_table, near_len, raw, prefill_rows, decode_rows
    )
    return (prefill_out, decode_out, received_pages)


def solution(mesh):
    placed = (
        P(("dp", "seq"), None),
        P(("dp", "seq"), None),
        P("dp", "seq"),
        P("dp", "seq"),
        P(),
        P("dp", None, "seq"),
        P("dp", None),
        P("dp"),
        P("dp"),
    )
    return jax.shard_map(
        on_device,
        mesh=mesh,
        in_specs=placed,
        out_specs=(P(("dp", "seq"), None), P("dp", "seq"), P("dp", None, "seq")),
        check_vma=False,
    )
```
